512 devices in a mesh: scen: 32 (over z, core), row: 16 (over x, y).
Axes of the slice: x: 4, y: 4, z: 16, core: 2. Of those that a mesh axis runs over, the one named last changes fastest.
Arguments:
- coupling: bfloat16 [32, 1536, 16384], P('scen', None, 'row'), may hold values from -40 to 40
- solves: bfloat16 [32, 1536, 512], P('scen', 'row'), may hold values from -0.625 to 0.625
- border_diagonal: float32 [1024, 16], P('scen', 'row'), may hold values from 32 to 64
- panel_rows: int32 [512], replicated, may hold values from 0 to 16383, as said below
Outputs:
- first_factor: float32 [1024, 16, 256], P('scen', 'row')
- second_factor: float32 [1024, 16, 256], P('scen', 'row')
The draws below stay inside these ranges and needn't reach their ends.
Inputs may be any that keep to these rules, and one draw needn't show every extreme that they name: `panel_rows`: 512 distinct border rows; the first 256 are the first panel's pivot rows and columns, the rest the second's.
All inputs are finite; a program needn't handle non-finite values. Where the reference program divides by a largest or mean magnitude, that divisor is 1e-20 or more.
Results may differ from the reference program's by a relative error of at most 0.0003.
Values may be sent and summed in bfloat16 or wider, within the bound.
A program may use at most 64 MiB of HBM per device.

```python
import math
import jax
import jax.numpy as jnp
from jax import lax

NLOC = 1536
HALF = 256
NEWTON = 8
ROW_DEV = 1024
PANEL = 512
SCENARIOS = 32
BORDER = 16384
N_ROW = 16


def pick_panel(key):
    key_pick = jax.random.fold_in(key, 11)
    key_order = jax.random.fold_in(key, 12)
    inner = jax.random.permutation(key_pick, BORDER - 2)[:PANEL - 2].astype(jnp.int32) + 1
    ends = jnp.array([0, BORDER - 1], dtype=jnp.int32)
    whole = jnp.concatenate([inner, ends])
    return whole[jax.random.permutation(key_order, PANEL)]


def draw_panel_rows(key, part):
    return pick_panel(key)


def draw_coupling(key, part):
    chosen = pick_panel(key)
    glob = jnp.arange(BORDER, dtype=jnp.int32)
    is_pivot = jnp.any(glob[:, None] == chosen[None, :], axis=1)
    key_scale = jax.random.fold_in(key, 21)
    key_value = jax.random.fold_in(key, 22)
    logs = jax.random.uniform(key_scale, (BORDER,), jnp.float32, jnp.log(64.0), jnp.log(256.0))
    column_scale = jnp.where(is_pivot, jnp.float32(1.0), jnp.exp(logs))
    values = jnp.clip(jax.random.normal(key_value, (SCENARIOS, NLOC, BORDER), jnp.float32), -6.0, 6.0)
    scaled = values * float(NLOC) ** (-0.5) * column_scale[None, None, :]
    scaled = jnp.clip(scaled, -40.0, 40.0)
    return scaled.astype(jnp.bfloat16)


def level_of(stream_key, shape, split, smallest, largest):
    def one(dim, blocks):
        steps = jax.random.uniform(jax.random.fold_in(jax.random.fold_in(stream_key, 6), dim), (blocks,), jnp.float32, smallest / len(split), largest / len(split))
        return jnp.repeat(jnp.exp(steps), shape[dim] // blocks).reshape((-1,) + (1,) * (len(shape) - dim - 1))

    factor_of = one(*split[0])
    for cut in split[1:]:
        factor_of = factor_of * one(*cut)
    return factor_of


def scatter_about(rng, dims, scale, bound, cuts=(), held_as=jnp.bfloat16):
    values = jax.random.normal(rng, dims, jnp.float32) * scale
    if len(cuts) > 0:
        values = level_of(rng, dims, cuts, -0.22, 0.18) * values
    return jnp.clip(values, min=-bound, max=bound).astype(held_as)


def setup_inputs(seed: int = 0) -> dict:
    keys = jax.random.split(jax.random.key(seed), 5)
    return {
        "coupling": draw_coupling(jax.random.fold_in(keys[4], 71), 0),
        "solves": scatter_about(keys[1], (SCENARIOS, NLOC, PANEL), (0.25 / SCENARIOS ** 0.5), 0.625, ((0, 32), (1, 16))),
        "border_diagonal": jnp.clip(jnp.exp(math.log(64.0) - 0.6931472 * jax.random.uniform(keys[2], (ROW_DEV, N_ROW), jnp.float32) ** level_of(keys[2], (ROW_DEV, N_ROW), ((0, 32), (1, 16)), -0.2, 0.2)), 32.0, 64.0),
        "panel_rows": draw_panel_rows(jax.random.fold_in(keys[4], 71), 0),
    }


def newton(pivot):
    norm_one = jnp.max(jnp.sum(jnp.abs(pivot), axis=0))
    norm_inf = jnp.max(jnp.sum(jnp.abs(pivot), axis=1))
    approx = pivot.T / (norm_one * norm_inf)
    for step in range(NEWTON):
        left = jnp.dot(approx, pivot, precision=lax.Precision.HIGHEST)
        approx = 2.0 * approx - jnp.dot(left, approx, precision=lax.Precision.HIGHEST)
    return approx


def reference(coupling, solves, border_diagonal, panel_rows):
    def add_one(total, pair):
        block, result = pair
        return total + jnp.dot(block.T, result, preferred_element_type=jnp.float32), None

    schur, unused = lax.scan(add_one, jnp.zeros((BORDER, PANEL), jnp.float32), (coupling, solves))
    glob = jnp.arange(BORDER, dtype=jnp.int32)
    diag_flat = border_diagonal.T.reshape(BORDER)
    schur = schur + jnp.where(glob[:, None] == panel_rows[None, :], diag_flat[:, None], jnp.float32(0.0))
    pivots = schur[panel_rows]
    inverse_first = newton(pivots[:HALF, :HALF])
    first_factor = jnp.dot(schur[:, :HALF], inverse_first, precision=lax.Precision.HIGHEST)
    updated = schur[:, HALF:] - jnp.dot(first_factor, pivots[:HALF, HALF:], precision=lax.Precision.HIGHEST)
    inverse_second = newton(updated[panel_rows[HALF:]])
    second_factor = jnp.dot(updated, inverse_second, precision=lax.Precision.HIGHEST)
    first_out = first_factor.reshape(N_ROW, ROW_DEV, HALF).transpose(1, 0, 2)
    second_out = second_factor.reshape(N_ROW, ROW_DEV, HALF).transpose(1, 0, 2)
    return first_out, second_out
```

```python
import jax
import jax.numpy as jnp
from jax import lax
from jax.sharding import PartitionSpec as P

HALF = 256
NEWTON = 8


def newton_start(pivot):
    norm_one = jnp.max(jnp.sum(jnp.abs(pivot), axis=0))
    norm_inf = jnp.max(jnp.sum(jnp.abs(pivot), axis=1))
    return pivot.T / (norm_one * norm_inf)


def invert(pivot):
    approx = newton_start(pivot)
    for step in range(NEWTON):
        left = jnp.dot(approx, pivot, precision=lax.Precision.HIGHEST)
        approx = 2.0 * approx - jnp.dot(left, approx, precision=lax.Precision.HIGHEST)
    return approx


def eliminate(both, pivots):
    first = both[:, :HALF]
    second = both[:, HALF:]
    inverse_first = invert(pivots[:HALF, :HALF])
    first_factor = jnp.dot(first, inverse_first, precision=lax.Precision.HIGHEST)
    upper = pivots[:HALF, HALF:]
    updated = second - jnp.dot(first_factor, upper, precision=lax.Precision.HIGHEST)
    lower_factor = jnp.dot(pivots[HALF:, :HALF], inverse_first, precision=lax.Precision.HIGHEST)
    pivot_two = pivots[HALF:, HALF:] - jnp.dot(
        lower_factor, upper, precision=lax.Precision.HIGHEST
    )
    inverse_second = invert(pivot_two)
    second_factor = jnp.dot(updated, inverse_second, precision=lax.Precision.HIGHEST)
    return (first_factor[:, None, :], second_factor[:, None, :])


def shards(coupling, solves, border_diagonal, panel_rows):
    scens = lax.axis_size("scen")
    full_solves = lax.all_gather(solves[0], "row", axis=0, tiled=True)
    row_count = coupling.shape[2]
    panel = panel_rows.shape[0]
    share = row_count // scens
    pivot_share = panel // scens
    first_row = lax.axis_index("row") * row_count
    base = first_row + lax.axis_index("scen") * share
    local = first_row + jnp.arange(row_count, dtype=jnp.int32)
    pick = (local[:, None] == panel_rows[None, :]).astype(jnp.bfloat16)
    chosen = jnp.dot(coupling[0], pick, preferred_element_type=jnp.float32).astype(jnp.bfloat16)
    glob = base + jnp.arange(share, dtype=jnp.int32)
    diag_part = jnp.where(
        glob[:, None] == panel_rows[None, :], border_diagonal[:, 0][:, None], jnp.float32(0.0)
    )
    main = jnp.einsum("nr,nc->rc", coupling[0], full_solves, preferred_element_type=jnp.float32)
    extra = jnp.einsum("nr,nc->rc", chosen, full_solves, preferred_element_type=jnp.float32)
    diag_row = jnp.sum(diag_part, axis=0)
    order = jnp.arange(panel, dtype=jnp.int32)
    extra = extra + jnp.where(order[:, None] == order[None, :], diag_row[:, None], jnp.float32(0.0))
    joined = jnp.concatenate(
        [main.reshape(scens, share, panel), extra.reshape(scens, pivot_share, panel)], axis=1
    ).reshape(scens * (share + pivot_share), panel)
    summed = lax.psum_scatter(joined, "scen", scatter_dimension=0, tiled=True)
    both = summed[:share] + diag_part
    pivots = lax.all_gather(lax.psum(summed[share:], "row"), "scen", axis=0, tiled=True)
    return eliminate(both, pivots)


def solution(mesh):
    placed = (P("scen", None, "row"), P("scen", "row", None), P("scen", "row"), P())
    return jax.shard_map(
        shards,
        mesh=mesh,
        in_specs=placed,
        out_specs=(P("scen", "row", None), P("scen", "row", None)),
        check_vma=False,
    )
```

```python
import jax
import jax.numpy as jnp
from jax import lax
from jax.experimental import pallas as pl
from jax.experimental.pallas import tpu as pltpu
from jax.sharding import PartitionSpec as P

HALF = 256
NEWTON = 8
GRID = 4
MESH = pl.DeviceIdType.MESH
VMEM = pl.BlockSpec(memory_space=pltpu.VMEM)


def greet(devices):
    barrier = pltpu.get_barrier_semaphore()
    for device in devices:
        pl.semaphore_signal(barrier, inc=1, device_id=device, device_id_type=MESH)
    pl.semaphore_wait(barrier, len(devices))


def gather_kernel(own_ref, out_ref, send_sem, recv_sem):
    me = lax.axis_index("row")
    x, y = me // GRID, me % GRID
    depth, width = own_ref.shape
    middle = depth // 2
    halves = ((0, width // 2), (width // 2, width // 2))

    def index(half, along, across):
        dx, dy = (across, along) if half == 0 else (along, across)
        return ((x + dx + GRID) % GRID) * GRID + (y + dy + GRID) % GRID

    greet([{"row": index(0, a, b)} for a, b in ((1, 0), (-1, 0), (0, 1), (0, -1))])
    out_ref[me] = own_ref[...]
    sent = []

    def view(half, owner, part):
        start, size = ((0, depth), (0, middle), (middle, depth - middle))[part]
        return out_ref.at[owner, pl.ds(start, size), pl.ds(*halves[half])]

    def copy(half, ring, kind, owner, own, target):
        part = (0, 0, 1, 2)[kind]
        slot = (half * 5 + ring) * 4 + kind
        there = view(half, owner, part)
        source = own_ref.at[:, pl.ds(*halves[half])] if own else there
        return pltpu.make_async_remote_copy(
            src_ref=source,
            dst_ref=there,
            send_sem=send_sem.at[slot],
            recv_sem=recv_sem.at[slot],
            device_id={"row": target},
            device_id_type=MESH,
        )

    def place(half, ring, q, step):
        return index(half, step, 0) if ring == 0 else index(half, q, step)

    def peer(half, ring, step):
        return index(half, step, 0) if ring == 0 else index(half, 0, step)

    def start(half, ring, q):
        for kind, step in ((0, 1), (1, -1)):
            one = copy(half, ring, kind, place(half, ring, q, 0), q == 0, peer(half, ring, step))
            one.start()
            sent.append(one)

    def relay(half, ring, q):
        for kind, step in ((0, 1), (1, -1)):
            copy(half, ring, kind, place(half, ring, q, -step), False, peer(half, ring, step)).wait_recv()
            one = copy(half, ring, kind + 2, place(half, ring, q, -step), False, peer(half, ring, step))
            one.start()
            sent.append(one)

    def finish(half, ring, q):
        for kind, step in ((2, 1), (3, -1)):
            copy(half, ring, kind, place(half, ring, q, 2), False, peer(half, ring, step)).wait_recv()

    order = ((1, 0), (2, -1), (3, 1), (4, 2))
    for half in range(2):
        start(half, 0, 0)
    for half in range(2):
        start(half, 1, 0)
    for half in range(2):
        relay(half, 0, 0)
        start(half, 2, -1)
        start(half, 3, 1)
    for half in range(2):
        relay(half, 1, 0)
    for half in range(2):
        finish(half, 0, 0)
        start(half, 4, 2)
    for ring, q in order[1:]:
        for half in range(2):
            relay(half, ring, q)
    for ring, q in order:
        for half in range(2):
            finish(half, ring, q)
    for one in sent:
        one.wait_send()


def gather_solves(own):
    depth, width = own.shape
    devices = GRID * GRID
    return pl.pallas_call(
        gather_kernel,
        out_shape=jax.ShapeDtypeStruct((devices, depth, width), own.dtype),
        in_specs=[VMEM],
        out_specs=VMEM,
        scratch_shapes=[pltpu.SemaphoreType.DMA((40,)), pltpu.SemaphoreType.DMA((40,))],
        compiler_params=pltpu.CompilerParams(collective_id=0, has_side_effects=True),
        name="gather_solves",
    )(own).reshape(devices * depth, width)


def reduce_kernel(
    main_ref, extra_ref, diag_ref, both_ref, pivot_ref,
    got_main, got_extra, acc_main, acc_extra,
    main_back, main_on, extra_back, extra_on, y_slots, x_slots, stage,
    send_sem, recv_sem,
):
    chips = main_ref.shape[0]
    far = chips // 2
    scen = lax.axis_index("scen")
    me = lax.axis_index("row")
    z, core = scen // 2, scen % 2
    x, y = me // GRID, me % GRID
    partner = {"scen": z * 2 + 1 - core}
    back = {"scen": ((z + chips - 1) % chips) * 2 + core}
    on = {"scen": ((z + 1) % chips) * 2 + core}
    y_peers = [{"row": x * GRID + (y + j) % GRID} for j in range(1, GRID)]
    x_peers = [{"row": ((x + j) % GRID) * GRID + y} for j in range(1, GRID)]
    greet([partner, back, on] + y_peers + x_peers)
    sent = []
    slots = iter(range(send_sem.shape[0]))

    def copy(source, there, slot, device):
        return pltpu.make_async_remote_copy(
            src_ref=source,
            dst_ref=there,
            send_sem=send_sem.at[slot],
            recv_sem=recv_sem.at[slot],
            device_id=device,
            device_id_type=MESH,
        )

    def send(source, there, slot, device):
        one = copy(source, there, slot, device)
        one.start()
        sent.append(one)
        return one

    swap_extra = send(extra_ref.at[:, 1 - core], got_extra, next(slots), partner)
    swap_main = send(main_ref.at[:, 1 - core], got_main, next(slots), partner)

    def ring(acc, back_slots, on_slots):
        back_ids = [next(slots) for _ in range(far)]
        on_ids = [next(slots) for _ in range(far - 1)]
        back_sent, on_sent = [], []

        def step(k):
            if k <= far:
                to = (z + far + k) % chips
                if k >= 1:
                    back_sent[k - 1].wait_recv()
                    acc[to] = acc[to] + back_slots[k - 1]
                if k < far:
                    back_sent.append(send(acc.at[to], back_slots.at[k], back_ids[k], back))
            if k <= far - 1:
                to = (z + far - 1 - k) % chips
                if k >= 1:
                    on_sent[k - 1].wait_recv()
                    acc[to] = acc[to] + on_slots[k - 1]
                if k < far - 1:
                    on_sent.append(send(acc.at[to], on_slots.at[k], on_ids[k], on))

        return step

    swap_extra.wait_recv()
    acc_extra[...] = extra_ref[:, core] + got_extra[...]
    extra_step = ring(acc_extra, extra_back, extra_on)
    main_step = ring(acc_main, main_back, main_on)
    extra_step(0)
    swap_main.wait_recv()
    acc_main[...] = main_ref[:, core] + got_main[...]
    for k in range(1, far + 1):
        extra_step(k)
    y_sent = [
        send(acc_extra.at[z], y_slots.at[j], next(slots), device) for j, device in enumerate(y_peers)
    ]
    main_step(0)
    for one in y_sent:
        one.wait_recv()
    stage[...] = (acc_extra[z] + y_slots[0]) + (y_slots[1] + y_slots[2])
    x_sent = [
        send(stage, x_slots.at[j], next(slots), device) for j, device in enumerate(x_peers)
    ]
    main_step(1)
    for one in x_sent:
        one.wait_recv()
    pivot_ref[z, core] = (stage[...] + x_slots[0]) + (x_slots[1] + x_slots[2])

    back_ids = [next(slots) for _ in range(far)]
    on_ids = [next(slots) for _ in range(far - 1)]
    share_ids = [next(slots) for _ in range(chips)]

    def block(offset, side):
        return pivot_ref.at[(z + offset + chips) % chips, side]

    def pass_back(k, offset):
        return copy(block(offset, core), block(offset, core), back_ids[k], back)

    def pass_on(k, offset):
        return copy(block(offset, core), block(offset, core), on_ids[k], on)

    def share(offset):
        send(block(offset, core), block(offset, core), share_ids[offset + far - 1], partner)

    def launch(one):
        one.start()
        sent.append(one)

    launch(pass_back(0, 0))
    launch(pass_on(0, 0))
    share(0)
    main_step(2)
    for k in range(1, far + 1):
        pass_back(k - 1, k).wait_recv()
        if k < far:
            launch(pass_back(k, k))
        if k < far:
            pass_on(k - 1, -k).wait_recv()
            if k < far - 1:
                launch(pass_on(k, -k))
            share(-k)
        share(k)
        if k + 2 <= far:
            main_step(k + 2)
    both_ref[...] = acc_main[z] + diag_ref[...]
    for offset in range(1 - far, far + 1):
        copy(
            block(offset, 1 - core), block(offset, 1 - core), share_ids[offset + far - 1], partner
        ).wait_recv()
    for one in sent:
        one.wait_send()


def reduce_and_share(main, extra, diag):
    rows, panel = main.shape
    scens = lax.axis_size("scen")
    chips = scens // 2
    far = chips // 2
    share, pivots = rows // scens, panel // scens
    f32 = jnp.float32
    count = 2 + 3 * (2 * far - 1) + 2 * (GRID - 1) + chips
    both, pivot = pl.pallas_call(
        reduce_kernel,
        out_shape=(
            jax.ShapeDtypeStruct((share, panel), f32),
            jax.ShapeDtypeStruct((chips, 2, pivots, panel), f32),
        ),
        in_specs=[VMEM] * 3,
        out_specs=(VMEM, VMEM),
        scratch_shapes=[
            pltpu.VMEM((chips, share, panel), f32),
            pltpu.VMEM((chips, pivots, panel), f32),
            pltpu.VMEM((chips, share, panel), f32),
            pltpu.VMEM((chips, pivots, panel), f32),
            pltpu.VMEM((far, share, panel), f32),
            pltpu.VMEM((far - 1, share, panel), f32),
            pltpu.VMEM((far, pivots, panel), f32),
            pltpu.VMEM((far - 1, pivots, panel), f32),
            pltpu.VMEM((GRID - 1, pivots, panel), f32),
            pltpu.VMEM((GRID - 1, pivots, panel), f32),
            pltpu.VMEM((pivots, panel), f32),
            pltpu.SemaphoreType.DMA((count,)),
            pltpu.SemaphoreType.DMA((count,)),
        ],
        compiler_params=pltpu.CompilerParams(collective_id=1, has_side_effects=True),
        name="reduce_and_share",
    )(main.reshape(chips, 2, share, panel), extra.reshape(chips, 2, pivots, panel), diag)
    return both, pivot.reshape(panel, panel)


def newton_start(pivot):
    norm_one = jnp.max(jnp.sum(jnp.abs(pivot), axis=0))
    norm_inf = jnp.max(jnp.sum(jnp.abs(pivot), axis=1))
    return pivot.T / (norm_one * norm_inf)


def invert(pivot):
    approx = newton_start(pivot)
    for step in range(NEWTON):
        left = jnp.dot(approx, pivot, precision=lax.Precision.HIGHEST)
        approx = 2.0 * approx - jnp.dot(left, approx, precision=lax.Precision.HIGHEST)
    return approx


def eliminate(both, pivots):
    first = both[:, :HALF]
    second = both[:, HALF:]
    inverse_first = invert(pivots[:HALF, :HALF])
    first_factor = jnp.dot(first, inverse_first, precision=lax.Precision.HIGHEST)
    upper = pivots[:HALF, HALF:]
    updated = second - jnp.dot(first_factor, upper, precision=lax.Precision.HIGHEST)
    lower_factor = jnp.dot(pivots[HALF:, :HALF], inverse_first, precision=lax.Precision.HIGHEST)
    pivot_two = pivots[HALF:, HALF:] - jnp.dot(
        lower_factor, upper, precision=lax.Precision.HIGHEST
    )
    inverse_second = invert(pivot_two)
    second_factor = jnp.dot(updated, inverse_second, precision=lax.Precision.HIGHEST)
    return (first_factor[:, None, :], second_factor[:, None, :])


def shards(coupling, solves, border_diagonal, panel_rows):
    scens = lax.axis_size("scen")
    full_solves = gather_solves(solves[0])
    row_count = coupling.shape[2]
    panel = panel_rows.shape[0]
    share = row_count // scens
    first_row = lax.axis_index("row") * row_count
    base = first_row + lax.axis_index("scen") * share
    local = first_row + jnp.arange(row_count, dtype=jnp.int32)
    pick = (local[:, None] == panel_rows[None, :]).astype(jnp.bfloat16)
    chosen = jnp.dot(coupling[0], pick, preferred_element_type=jnp.float32).astype(jnp.bfloat16)
    glob = base + jnp.arange(share, dtype=jnp.int32)
    diag_part = jnp.where(
        glob[:, None] == panel_rows[None, :], border_diagonal[:, 0][:, None], jnp.float32(0.0)
    )
    main = jnp.einsum("nr,nc->rc", coupling[0], full_solves, preferred_element_type=jnp.float32)
    extra = jnp.einsum("nr,nc->rc", chosen, full_solves, preferred_element_type=jnp.float32)
    diag_row = jnp.sum(diag_part, axis=0)
    order = jnp.arange(panel, dtype=jnp.int32)
    extra = extra + jnp.where(order[:, None] == order[None, :], diag_row[:, None], jnp.float32(0.0))
    both, pivots = reduce_and_share(main, extra, diag_part)
    return eliminate(both, pivots)


def solution(mesh):
    placed = (P("scen", None, "row"), P("scen", "row", None), P("scen", "row"), P())
    return jax.shard_map(
        shards,
        mesh=mesh,
        in_specs=placed,
        out_specs=(P("scen", "row", None), P("scen", "row", None)),
        check_vma=False,
    )
```

```python
import jax
import jax.numpy as jnp
from jax import lax
from jax.experimental import pallas as pl
from jax.experimental.pallas import tpu as pltpu
from jax.sharding import PartitionSpec as P

HALF = 256
NEWTON = 8
GRID = 4
MESH = pl.DeviceIdType.MESH
VMEM = pl.BlockSpec(memory_space=pltpu.VMEM)


def greet(devices):
    barrier = pltpu.get_barrier_semaphore()
    for device in devices:
        pl.semaphore_signal(barrier, inc=1, device_id=device, device_id_type=MESH)
    pl.semaphore_wait(barrier, len(devices))


def gather_kernel(own_ref, out_ref, send_sem, recv_sem):
    me = lax.axis_index("row")
    x, y = me // GRID, me % GRID
    depth, width = own_ref.shape
    middle = depth // 2
    halves = ((0, width // 2), (width // 2, width // 2))

    def index(half, along, across):
        dx, dy = (across, along) if half == 0 else (along, across)
        return ((x + dx + GRID) % GRID) * GRID + (y + dy + GRID) % GRID

    greet([{"row": index(0, a, b)} for a, b in ((1, 0), (-1, 0), (0, 1), (0, -1))])
    out_ref[me] = own_ref[...]
    sent = []

    def view(half, owner, part):
        start, size = ((0, depth), (0, middle), (middle, depth - middle))[part]
        return out_ref.at[owner, pl.ds(start, size), pl.ds(*halves[half])]

    def copy(half, ring, kind, owner, own, target):
        part = (0, 0, 1, 2)[kind]
        slot = (half * 5 + ring) * 4 + kind
        there = view(half, owner, part)
        source = own_ref.at[:, pl.ds(*halves[half])] if own else there
        return pltpu.make_async_remote_copy(
            src_ref=source,
            dst_ref=there,
            send_sem=send_sem.at[slot],
            recv_sem=recv_sem.at[slot],
            device_id={"row": target},
            device_id_type=MESH,
        )

    def place(half, ring, q, step):
        return index(half, step, 0) if ring == 0 else index(half, q, step)

    def peer(half, ring, step):
        return index(half, step, 0) if ring == 0 else index(half, 0, step)

    def start(half, ring, q):
        for kind, step in ((0, 1), (1, -1)):
            one = copy(half, ring, kind, place(half, ring, q, 0), q == 0, peer(half, ring, step))
            one.start()
            sent.append(one)

    def relay(half, ring, q):
        for kind, step in ((0, 1), (1, -1)):
            copy(half, ring, kind, place(half, ring, q, -step), False, peer(half, ring, step)).wait_recv()
            one = copy(half, ring, kind + 2, place(half, ring, q, -step), False, peer(half, ring, step))
            one.start()
            sent.append(one)

    def finish(half, ring, q):
        for kind, step in ((2, 1), (3, -1)):
            copy(half, ring, kind, place(half, ring, q, 2), False, peer(half, ring, step)).wait_recv()

    order = ((1, 0), (2, -1), (3, 1), (4, 2))
    for half in range(2):
        start(half, 0, 0)
    for half in range(2):
        start(half, 1, 0)
    for half in range(2):
        relay(half, 0, 0)
        start(half, 2, -1)
        start(half, 3, 1)
    for half in range(2):
        relay(half, 1, 0)
    for half in range(2):
        finish(half, 0, 0)
        start(half, 4, 2)
    for ring, q in order[1:]:
        for half in range(2):
            relay(half, ring, q)
    for ring, q in order:
        for half in range(2):
            finish(half, ring, q)
    for one in sent:
        one.wait_send()


def gather_solves(own):
    depth, width = own.shape
    devices = GRID * GRID
    return pl.pallas_call(
        gather_kernel,
        out_shape=jax.ShapeDtypeStruct((devices, depth, width), own.dtype),
        in_specs=[VMEM],
        out_specs=VMEM,
        scratch_shapes=[pltpu.SemaphoreType.DMA((40,)), pltpu.SemaphoreType.DMA((40,))],
        compiler_params=pltpu.CompilerParams(collective_id=0, has_side_effects=True),
        name="gather_solves",
    )(own).reshape(devices * depth, width)


def reduce_kernel(
    main_ref, extra_ref, diag_ref, both_ref, pivot_ref,
    got_main, got_extra, acc_main, acc_extra,
    main_back, main_on, extra_back, extra_on, y_slots, x_slots, stage,
    send_sem, recv_sem,
):
    chips = main_ref.shape[0]
    far = chips // 2
    scen = lax.axis_index("scen")
    me = lax.axis_index("row")
    z, core = scen // 2, scen % 2
    x, y = me // GRID, me % GRID
    partner = {"scen": z * 2 + 1 - core}
    back = {"scen": ((z + chips - 1) % chips) * 2 + core}
    on = {"scen": ((z + 1) % chips) * 2 + core}
    y_peers = [{"row": x * GRID + (y + j) % GRID} for j in range(1, GRID)]
    x_peers = [{"row": ((x + j) % GRID) * GRID + y} for j in range(1, GRID)]
    greet([partner, back, on] + y_peers + x_peers)
    sent = []
    slots = iter(range(send_sem.shape[0]))

    def copy(source, there, slot, device):
        return pltpu.make_async_remote_copy(
            src_ref=source,
            dst_ref=there,
            send_sem=send_sem.at[slot],
            recv_sem=recv_sem.at[slot],
            device_id=device,
            device_id_type=MESH,
        )

    def send(source, there, slot, device):
        one = copy(source, there, slot, device)
        one.start()
        sent.append(one)
        return one

    swap_extra = send(extra_ref.at[:, 1 - core], got_extra, next(slots), partner)
    swap_main = send(main_ref.at[:, 1 - core], got_main, next(slots), partner)

    def ring(acc, back_slots, on_slots):
        back_ids = [next(slots) for _ in range(far)]
        on_ids = [next(slots) for _ in range(far - 1)]
        back_sent, on_sent = [], []

        def step(k):
            if k <= far:
                to = (z + far + k) % chips
                if k >= 1:
                    back_sent[k - 1].wait_recv()
                    acc[to] = acc[to] + back_slots[k - 1]
                if k < far:
                    back_sent.append(send(acc.at[to], back_slots.at[k], back_ids[k], back))
            if k <= far - 1:
                to = (z + far - 1 - k) % chips
                if k >= 1:
                    on_sent[k - 1].wait_recv()
                    acc[to] = acc[to] + on_slots[k - 1]
                if k < far - 1:
                    on_sent.append(send(acc.at[to], on_slots.at[k], on_ids[k], on))

        return step

    swap_extra.wait_recv()
    acc_extra[...] = extra_ref[:, core] + got_extra[...]
    extra_step = ring(acc_extra, extra_back, extra_on)
    main_step = ring(acc_main, main_back, main_on)
    extra_step(0)
    swap_main.wait_recv()
    acc_main[...] = main_ref[:, core] + got_main[...]
    for k in range(1, far + 1):
        extra_step(k)
    y_sent = [
        send(acc_extra.at[z], y_slots.at[j], next(slots), device) for j, device in enumerate(y_peers)
    ]
    main_step(0)
    for one in y_sent:
        one.wait_recv()
    stage[...] = (acc_extra[z] + y_slots[0]) + (y_slots[1] + y_slots[2])
    x_sent = [
        send(stage, x_slots.at[j], next(slots), device) for j, device in enumerate(x_peers)
    ]
    main_step(1)
    for one in x_sent:
        one.wait_recv()
    pivot_ref[z, core] = (stage[...] + x_slots[0]) + (x_slots[1] + x_slots[2])

    back_ids = [next(slots) for _ in range(far)]
    on_ids = [next(slots) for _ in range(far - 1)]
    share_ids = [next(slots) for _ in range(chips)]

    def block(offset, side):
        return pivot_ref.at[(z + offset + chips) % chips, side]

    def pass_back(k, offset):
        return copy(block(offset, core), block(offset, core), back_ids[k], back)

    def pass_on(k, offset):
        return copy(block(offset, core), block(offset, core), on_ids[k], on)

    def share(offset):
        send(block(offset, core), block(offset, core), share_ids[offset + far - 1], partner)

    def launch(one):
        one.start()
        sent.append(one)

    launch(pass_back(0, 0))
    launch(pass_on(0, 0))
    share(0)
    main_step(2)
    for k in range(1, far + 1):
        pass_back(k - 1, k).wait_recv()
        if k < far:
            launch(pass_back(k, k))
        if k < far:
            pass_on(k - 1, -k).wait_recv()
            if k < far - 1:
                launch(pass_on(k, -k))
            share(-k)
        share(k)
        if k + 2 <= far:
            main_step(k + 2)
    both_ref[...] = acc_main[z] + diag_ref[...]
    for offset in range(1 - far, far + 1):
        copy(
            block(offset, 1 - core), block(offset, 1 - core), share_ids[offset + far - 1], partner
        ).wait_recv()
    for one in sent:
        one.wait_send()


def reduce_and_share(main, extra, diag):
    rows, panel = main.shape
    scens = lax.axis_size("scen")
    chips = scens // 2
    far = chips // 2
    share, pivots = rows // scens, panel // scens
    f32 = jnp.float32
    count = 2 + 3 * (2 * far - 1) + 2 * (GRID - 1) + chips
    both, pivot = pl.pallas_call(
        reduce_kernel,
        out_shape=(
            jax.ShapeDtypeStruct((share, panel), f32),
            jax.ShapeDtypeStruct((chips, 2, pivots, panel), f32),
        ),
        in_specs=[VMEM] * 3,
        out_specs=(VMEM, VMEM),
        scratch_shapes=[
            pltpu.VMEM((chips, share, panel), f32),
            pltpu.VMEM((chips, pivots, panel), f32),
            pltpu.VMEM((chips, share, panel), f32),
            pltpu.VMEM((chips, pivots, panel), f32),
            pltpu.VMEM((far, share, panel), f32),
            pltpu.VMEM((far - 1, share, panel), f32),
            pltpu.VMEM((far, pivots, panel), f32),
            pltpu.VMEM((far - 1, pivots, panel), f32),
            pltpu.VMEM((GRID - 1, pivots, panel), f32),
            pltpu.VMEM((GRID - 1, pivots, panel), f32),
            pltpu.VMEM((pivots, panel), f32),
            pltpu.SemaphoreType.DMA((count,)),
            pltpu.SemaphoreType.DMA((count,)),
        ],
        compiler_params=pltpu.CompilerParams(collective_id=1, has_side_effects=True),
        name="reduce_and_share",
    )(main.reshape(chips, 2, share, panel), extra.reshape(chips, 2, pivots, panel), diag)
    return both, pivot.reshape(panel, panel)


def exact(a, b):
    return jnp.dot(a, b, precision=lax.Precision.HIGHEST, preferred_element_type=jnp.float32)


def split(a):
    high = a.astype(jnp.bfloat16)
    return high, (a - high.astype(jnp.float32)).astype(jnp.bfloat16)


def split_dot(a, b):
    def dot(p, q):
        return jnp.dot(p, q, preferred_element_type=jnp.float32)

    return dot(a[0], b[0]) + (dot(a[0], b[1]) + dot(a[1], b[0]))


def invert(pivot, approx_ref):
    size = jnp.abs(pivot)
    norm_one = jnp.max(jnp.sum(size, axis=0, keepdims=True), axis=1, keepdims=True)
    norm_inf = jnp.max(jnp.sum(size, axis=1, keepdims=True), axis=0, keepdims=True)
    approx_ref[...] = pivot.T / (norm_one * norm_inf)
    parts = split(pivot)

    def step(_, carry):
        approx = approx_ref[...]
        both = split(approx)
        left = split(split_dot(both, parts))
        approx_ref[...] = 2.0 * approx - split_dot(left, both)
        return carry

    lax.fori_loop(0, NEWTON - 1, step, 0)
    approx = approx_ref[...]
    return 2.0 * approx - exact(exact(approx, pivot), approx)


def eliminate_kernel(both_ref, pivot_ref, first_ref, second_ref, approx_ref):
    inverse_first = invert(pivot_ref[:HALF, :HALF], approx_ref)
    upper = pivot_ref[:HALF, HALF:]
    first = exact(both_ref[:, :HALF], inverse_first)
    first_ref[...] = first
    lower = exact(pivot_ref[HALF:, :HALF], inverse_first)
    pivot_two = pivot_ref[HALF:, HALF:] - exact(lower, upper)
    updated = both_ref[:, HALF:] - exact(first, upper)
    second_ref[...] = exact(updated, invert(pivot_two, approx_ref))


def eliminate(both, pivots):
    half = jax.ShapeDtypeStruct((both.shape[0], HALF), jnp.float32)
    first, second = pl.pallas_call(
        eliminate_kernel,
        out_shape=(half, half),
        in_specs=[VMEM, VMEM],
        out_specs=(VMEM, VMEM),
        scratch_shapes=[pltpu.VMEM((HALF, HALF), jnp.float32)],
        name="eliminate",
    )(both, pivots)
    return first[:, None, :], second[:, None, :]


def shards(coupling, solves, border_diagonal, panel_rows):
    scens = lax.axis_size("scen")
    full_solves = gather_solves(solves[0])
    row_count = coupling.shape[2]
    panel = panel_rows.shape[0]
    share = row_count // scens
    first_row = lax.axis_index("row") * row_count
    base = first_row + lax.axis_index("scen") * share
    local = first_row + jnp.arange(row_count, dtype=jnp.int32)
    pick = (local[:, None] == panel_rows[None, :]).astype(jnp.bfloat16)
    chosen = jnp.dot(coupling[0], pick, preferred_element_type=jnp.float32).astype(jnp.bfloat16)
    glob = base + jnp.arange(share, dtype=jnp.int32)
    diag_part = jnp.where(
        glob[:, None] == panel_rows[None, :], border_diagonal[:, 0][:, None], jnp.float32(0.0)
    )
    main = jnp.einsum("nr,nc->rc", coupling[0], full_solves, preferred_element_type=jnp.float32)
    extra = jnp.einsum("nr,nc->rc", chosen, full_solves, preferred_element_type=jnp.float32)
    diag_row = jnp.sum(diag_part, axis=0)
    order = jnp.arange(panel, dtype=jnp.int32)
    extra = extra + jnp.where(order[:, None] == order[None, :], diag_row[:, None], jnp.float32(0.0))
    both, pivots = reduce_and_share(main, extra, diag_part)
    return eliminate(both, pivots)


def solution(mesh):
    placed = (P("scen", None, "row"), P("scen", "row", None), P("scen", "row"), P())
    return jax.shard_map(
        shards,
        mesh=mesh,
        in_specs=placed,
        out_specs=(P("scen", "row", None), P("scen", "row", None)),
        check_vma=False,
    )
```

```python
import jax
import jax.numpy as jnp
from jax import lax
from jax.experimental import pallas as pl
from jax.experimental.pallas import tpu as pltpu
from jax.sharding import PartitionSpec as P

HALF = 256
NEWTON = 8
GRID = 4
MIB = 1 << 20
MESH = pl.DeviceIdType.MESH
VMEM = pl.BlockSpec(memory_space=pltpu.VMEM)


def greet(devices):
    barrier = pltpu.get_barrier_semaphore()
    for device in devices:
        pl.semaphore_signal(barrier, inc=1, device_id=device, device_id_type=MESH)
    pl.semaphore_wait(barrier, len(devices))


def gather_kernel(own_ref, out_ref, send_sem, recv_sem):
    me = lax.axis_index("row")
    x, y = me // GRID, me % GRID
    depth, width = own_ref.shape
    middle = depth // 2
    halves = ((0, width // 2), (width // 2, width // 2))

    def index(half, along, across):
        dx, dy = (across, along) if half == 0 else (along, across)
        return ((x + dx + GRID) % GRID) * GRID + (y + dy + GRID) % GRID

    greet([{"row": index(0, a, b)} for a, b in ((1, 0), (-1, 0), (0, 1), (0, -1))])
    out_ref[me] = own_ref[...]
    sent = []

    def view(half, owner, part):
        start, size = ((0, depth), (0, middle), (middle, depth - middle))[part]
        return out_ref.at[owner, pl.ds(start, size), pl.ds(*halves[half])]

    def copy(half, ring, kind, owner, own, target):
        part = (0, 0, 1, 2)[kind]
        slot = (half * 5 + ring) * 4 + kind
        there = view(half, owner, part)
        source = own_ref.at[:, pl.ds(*halves[half])] if own else there
        return pltpu.make_async_remote_copy(
            src_ref=source,
            dst_ref=there,
            send_sem=send_sem.at[slot],
            recv_sem=recv_sem.at[slot],
            device_id={"row": target},
            device_id_type=MESH,
        )

    def place(half, ring, q, step):
        return index(half, step, 0) if ring == 0 else index(half, q, step)

    def peer(half, ring, step):
        return index(half, step, 0) if ring == 0 else index(half, 0, step)

    def start(half, ring, q):
        for kind, step in ((0, 1), (1, -1)):
            one = copy(half, ring, kind, place(half, ring, q, 0), q == 0, peer(half, ring, step))
            one.start()
            sent.append(one)

    def relay(half, ring, q):
        for kind, step in ((0, 1), (1, -1)):
            copy(half, ring, kind, place(half, ring, q, -step), False, peer(half, ring, step)).wait_recv()
            one = copy(half, ring, kind + 2, place(half, ring, q, -step), False, peer(half, ring, step))
            one.start()
            sent.append(one)

    def finish(half, ring, q):
        for kind, step in ((2, 1), (3, -1)):
            copy(half, ring, kind, place(half, ring, q, 2), False, peer(half, ring, step)).wait_recv()

    order = ((1, 0), (2, -1), (3, 1), (4, 2))
    for half in range(2):
        start(half, 0, 0)
    for half in range(2):
        start(half, 1, 0)
    for half in range(2):
        relay(half, 0, 0)
        start(half, 2, -1)
        start(half, 3, 1)
    for half in range(2):
        relay(half, 1, 0)
    for half in range(2):
        finish(half, 0, 0)
        start(half, 4, 2)
    for ring, q in order[1:]:
        for half in range(2):
            relay(half, ring, q)
    for ring, q in order:
        for half in range(2):
            finish(half, ring, q)
    for one in sent:
        one.wait_send()


def gather_solves(own):
    depth, width = own.shape
    devices = GRID * GRID
    return pl.pallas_call(
        gather_kernel,
        out_shape=jax.ShapeDtypeStruct((devices, depth, width), own.dtype),
        in_specs=[VMEM],
        out_specs=VMEM,
        scratch_shapes=[pltpu.SemaphoreType.DMA((40,)), pltpu.SemaphoreType.DMA((40,))],
        compiler_params=pltpu.CompilerParams(
            collective_id=0, has_side_effects=True, vmem_limit_bytes=8 * MIB
        ),
        name="gather_solves",
    )(own).reshape(devices * depth, width)


def reduce_kernel(
    main_ref, extra_ref, diag_ref, both_ref, pivot_ref,
    got_main, got_extra, acc_main, acc_extra,
    main_back, main_on, extra_back, extra_on, y_slots, x_slots, stage,
    send_sem, recv_sem,
):
    chips = main_ref.shape[0]
    far = chips // 2
    scen = lax.axis_index("scen")
    me = lax.axis_index("row")
    z, core = scen // 2, scen % 2
    x, y = me // GRID, me % GRID
    partner = {"scen": z * 2 + 1 - core}
    back = {"scen": ((z + chips - 1) % chips) * 2 + core}
    on = {"scen": ((z + 1) % chips) * 2 + core}
    y_peers = [{"row": x * GRID + (y + j) % GRID} for j in range(1, GRID)]
    x_peers = [{"row": ((x + j) % GRID) * GRID + y} for j in range(1, GRID)]
    greet([partner, back, on] + y_peers + x_peers)
    sent = []
    slots = iter(range(send_sem.shape[0]))

    def copy(source, there, slot, device):
        return pltpu.make_async_remote_copy(
            src_ref=source,
            dst_ref=there,
            send_sem=send_sem.at[slot],
            recv_sem=recv_sem.at[slot],
            device_id=device,
            device_id_type=MESH,
        )

    def send(source, there, slot, device):
        one = copy(source, there, slot, device)
        one.start()
        sent.append(one)
        return one

    swap_extra = send(extra_ref.at[:, 1 - core], got_extra, next(slots), partner)
    swap_main = send(main_ref.at[:, 1 - core], got_main, next(slots), partner)

    def ring(acc, back_slots, on_slots):
        back_ids = [next(slots) for _ in range(far)]
        on_ids = [next(slots) for _ in range(far - 1)]
        back_sent, on_sent = [], []

        def step(k):
            if k <= far:
                to = (z + far + k) % chips
                if k >= 1:
                    back_sent[k - 1].wait_recv()
                    acc[to] = acc[to] + back_slots[k - 1]
                if k < far:
                    back_sent.append(send(acc.at[to], back_slots.at[k], back_ids[k], back))
            if k <= far - 1:
                to = (z + far - 1 - k) % chips
                if k >= 1:
                    on_sent[k - 1].wait_recv()
                    acc[to] = acc[to] + on_slots[k - 1]
                if k < far - 1:
                    on_sent.append(send(acc.at[to], on_slots.at[k], on_ids[k], on))

        return step

    swap_extra.wait_recv()
    acc_extra[...] = extra_ref[:, core] + got_extra[...]
    extra_step = ring(acc_extra, extra_back, extra_on)
    main_step = ring(acc_main, main_back, main_on)
    extra_step(0)
    swap_main.wait_recv()
    acc_main[...] = main_ref[:, core] + got_main[...]
    for k in range(1, far + 1):
        extra_step(k)
    y_sent = [
        send(acc_extra.at[z], y_slots.at[j], next(slots), device) for j, device in enumerate(y_peers)
    ]
    main_step(0)
    for one in y_sent:
        one.wait_recv()
    stage[...] = (acc_extra[z] + y_slots[0]) + (y_slots[1] + y_slots[2])
    x_sent = [
        send(stage, x_slots.at[j], next(slots), device) for j, device in enumerate(x_peers)
    ]
    main_step(1)
    for one in x_sent:
        one.wait_recv()
    pivot_ref[z, core] = (stage[...] + x_slots[0]) + (x_slots[1] + x_slots[2])

    back_ids = [next(slots) for _ in range(far)]
    on_ids = [next(slots) for _ in range(far - 1)]
    share_ids = [next(slots) for _ in range(chips)]

    def block(offset, side):
        return pivot_ref.at[(z + offset + chips) % chips, side]

    def pass_back(k, offset):
        return copy(block(offset, core), block(offset, core), back_ids[k], back)

    def pass_on(k, offset):
        return copy(block(offset, core), block(offset, core), on_ids[k], on)

    def share(offset):
        send(block(offset, core), block(offset, core), share_ids[offset + far - 1], partner)

    def launch(one):
        one.start()
        sent.append(one)

    launch(pass_back(0, 0))
    launch(pass_on(0, 0))
    share(0)
    main_step(2)
    for k in range(1, far + 1):
        pass_back(k - 1, k).wait_recv()
        if k < far:
            launch(pass_back(k, k))
        if k < far:
            pass_on(k - 1, -k).wait_recv()
            if k < far - 1:
                launch(pass_on(k, -k))
            share(-k)
        share(k)
        if k + 2 <= far:
            main_step(k + 2)
    both_ref[...] = acc_main[z] + diag_ref[...]
    for offset in range(1 - far, far + 1):
        copy(
            block(offset, 1 - core), block(offset, 1 - core), share_ids[offset + far - 1], partner
        ).wait_recv()
    for one in sent:
        one.wait_send()


def reduce_and_share(main, extra, diag):
    rows, panel = main.shape
    scens = lax.axis_size("scen")
    chips = scens // 2
    far = chips // 2
    share, pivots = rows // scens, panel // scens
    f32 = jnp.float32
    count = 2 + 3 * (2 * far - 1) + 2 * (GRID - 1) + chips
    both, pivot = pl.pallas_call(
        reduce_kernel,
        out_shape=(
            jax.ShapeDtypeStruct((share, panel), f32),
            jax.ShapeDtypeStruct((chips, 2, pivots, panel), f32),
        ),
        in_specs=[VMEM] * 3,
        out_specs=(VMEM, VMEM),
        scratch_shapes=[
            pltpu.VMEM((chips, share, panel), f32),
            pltpu.VMEM((chips, pivots, panel), f32),
            pltpu.VMEM((chips, share, panel), f32),
            pltpu.VMEM((chips, pivots, panel), f32),
            pltpu.VMEM((far, share, panel), f32),
            pltpu.VMEM((far - 1, share, panel), f32),
            pltpu.VMEM((far, pivots, panel), f32),
            pltpu.VMEM((far - 1, pivots, panel), f32),
            pltpu.VMEM((GRID - 1, pivots, panel), f32),
            pltpu.VMEM((GRID - 1, pivots, panel), f32),
            pltpu.VMEM((pivots, panel), f32),
            pltpu.SemaphoreType.DMA((count,)),
            pltpu.SemaphoreType.DMA((count,)),
        ],
        compiler_params=pltpu.CompilerParams(
            collective_id=1, has_side_effects=True, vmem_limit_bytes=16 * MIB
        ),
        name="reduce_and_share",
    )(main.reshape(chips, 2, share, panel), extra.reshape(chips, 2, pivots, panel), diag)
    return both, pivot.reshape(panel, panel)


def exact(a, b):
    return jnp.dot(a, b, precision=lax.Precision.HIGHEST, preferred_element_type=jnp.float32)


def split(a):
    high = a.astype(jnp.bfloat16)
    return high, (a - high.astype(jnp.float32)).astype(jnp.bfloat16)


def split_dot(a, b):
    def dot(p, q):
        return jnp.dot(p, q, preferred_element_type=jnp.float32)

    return dot(a[0], b[0]) + (dot(a[0], b[1]) + dot(a[1], b[0]))


def invert(pivot, approx_ref):
    size = jnp.abs(pivot)
    norm_one = jnp.max(jnp.sum(size, axis=0, keepdims=True), axis=1, keepdims=True)
    norm_inf = jnp.max(jnp.sum(size, axis=1, keepdims=True), axis=0, keepdims=True)
    approx_ref[...] = pivot.T / (norm_one * norm_inf)
    parts = split(pivot)

    def step(_, carry):
        approx = approx_ref[...]
        both = split(approx)
        left = split(split_dot(both, parts))
        approx_ref[...] = 2.0 * approx - split_dot(left, both)
        return carry

    lax.fori_loop(0, NEWTON - 1, step, 0)
    approx = approx_ref[...]
    return 2.0 * approx - exact(exact(approx, pivot), approx)


def eliminate_kernel(both_ref, pivot_ref, first_ref, second_ref, approx_ref):
    inverse_first = invert(pivot_ref[:HALF, :HALF], approx_ref)
    upper = pivot_ref[:HALF, HALF:]
    first = exact(both_ref[:, :HALF], inverse_first)
    first_ref[...] = first[:, None, :]
    lower = exact(pivot_ref[HALF:, :HALF], inverse_first)
    pivot_two = pivot_ref[HALF:, HALF:] - exact(lower, upper)
    updated = both_ref[:, HALF:] - exact(first, upper)
    second_ref[...] = exact(updated, invert(pivot_two, approx_ref))[:, None, :]


def eliminate(both, pivots):
    half = jax.ShapeDtypeStruct((both.shape[0], 1, HALF), jnp.float32)
    return pl.pallas_call(
        eliminate_kernel,
        out_shape=(half, half),
        in_specs=[VMEM, VMEM],
        out_specs=(VMEM, VMEM),
        scratch_shapes=[pltpu.VMEM((HALF, HALF), jnp.float32)],
        compiler_params=pltpu.CompilerParams(vmem_limit_bytes=16 * MIB),
        name="eliminate",
    )(both, pivots)


TILE = 256


def product_kernel(coupling_ref, solves_ref, pick_ref, main_ref, extra_ref, chosen_ref):
    depth, rows = coupling_ref.shape
    panel = solves_ref.shape[1]

    def dot(a, b):
        return jnp.dot(a, b, preferred_element_type=jnp.float32)

    def across(a, b):
        return lax.dot_general(a, b, (((0,), (0,)), ((), ())), preferred_element_type=jnp.float32)

    for at in range(0, depth, TILE):
        part = pl.ds(at, TILE)
        chosen_ref[part, :] = dot(coupling_ref[part, :], pick_ref[...]).astype(jnp.bfloat16)
    for at in range(0, panel, TILE):
        part = pl.ds(at, TILE)
        extra_ref[part, :] = across(chosen_ref[:, part], solves_ref[...])
    for at in range(0, rows, TILE):
        part = pl.ds(at, TILE)
        main_ref[part, :] = across(coupling_ref[:, part], solves_ref[...])


def products(coupling, full_solves, pick):
    depth, rows = coupling.shape
    panel = full_solves.shape[1]
    return pl.pallas_call(
        product_kernel,
        out_shape=(
            jax.ShapeDtypeStruct((rows, panel), jnp.float32),
            jax.ShapeDtypeStruct((panel, panel), jnp.float32),
        ),
        in_specs=[VMEM] * 3,
        out_specs=(VMEM, VMEM),
        scratch_shapes=[pltpu.VMEM((depth, panel), jnp.bfloat16)],
        compiler_params=pltpu.CompilerParams(vmem_limit_bytes=28 * MIB),
        name="products",
    )(coupling, full_solves, pick)


def shards(coupling, solves, border_diagonal, panel_rows):
    scens = lax.axis_size("scen")
    full_solves = gather_solves(solves[0])
    row_count = coupling.shape[2]
    panel = panel_rows.shape[0]
    share = row_count // scens
    first_row = lax.axis_index("row") * row_count
    base = first_row + lax.axis_index("scen") * share
    local = first_row + jnp.arange(row_count, dtype=jnp.int32)
    pick = (local[:, None] == panel_rows[None, :]).astype(jnp.bfloat16)
    glob = base + jnp.arange(share, dtype=jnp.int32)
    diag_part = jnp.where(
        glob[:, None] == panel_rows[None, :], border_diagonal[:, 0][:, None], jnp.float32(0.0)
    )
    main, extra = products(coupling[0], full_solves, pick)
    diag_row = jnp.sum(diag_part, axis=0)
    order = jnp.arange(panel, dtype=jnp.int32)
    extra = extra + jnp.where(order[:, None] == order[None, :], diag_row[:, None], jnp.float32(0.0))
    both, pivots = reduce_and_share(main, extra, diag_part)
    return eliminate(both, pivots)


def solution(mesh):
    placed = (P("scen", None, "row"), P("scen", "row", None), P("scen", "row"), P())
    return jax.shard_map(
        shards,
        mesh=mesh,
        in_specs=placed,
        out_specs=(P("scen", "row", None), P("scen", "row", None)),
        check_vma=False,
    )
```

```python
import jax
import jax.numpy as jnp
from jax import lax
from jax.experimental import pallas as pl
from jax.experimental.pallas import tpu as pltpu
from jax.sharding import PartitionSpec as P

HALF = 256
NEWTON = 8
GRID = 4
MIB = 1 << 20
MESH = pl.DeviceIdType.MESH
VMEM = pl.BlockSpec(memory_space=pltpu.VMEM)


def greet(devices):
    barrier = pltpu.get_barrier_semaphore()
    for device in devices:
        pl.semaphore_signal(barrier, inc=1, device_id=device, device_id_type=MESH)
    pl.semaphore_wait(barrier, len(devices))


def gather_kernel(own_ref, out_ref, send_sem, recv_sem):
    me = lax.axis_index("row")
    x, y = me // GRID, me % GRID
    depth, width = own_ref.shape
    middle = depth // 2
    halves = ((0, width // 2), (width // 2, width // 2))

    def index(half, along, across):
        dx, dy = (across, along) if half == 0 else (along, across)
        return ((x + dx + GRID) % GRID) * GRID + (y + dy + GRID) % GRID

    greet([{"row": index(0, a, b)} for a, b in ((1, 0), (-1, 0), (0, 1), (0, -1))])
    out_ref[me] = own_ref[...]
    sent = []

    def view(half, owner, part):
        start, size = ((0, depth), (0, middle), (middle, depth - middle))[part]
        return out_ref.at[owner, pl.ds(start, size), pl.ds(*halves[half])]

    def copy(half, ring, kind, owner, own, target):
        part = (0, 0, 1, 2)[kind]
        slot = (half * 5 + ring) * 4 + kind
        there = view(half, owner, part)
        source = own_ref.at[:, pl.ds(*halves[half])] if own else there
        return pltpu.make_async_remote_copy(
            src_ref=source,
            dst_ref=there,
            send_sem=send_sem.at[slot],
            recv_sem=recv_sem.at[slot],
            device_id={"row": target},
            device_id_type=MESH,
        )

    def place(half, ring, q, step):
        return index(half, step, 0) if ring == 0 else index(half, q, step)

    def peer(half, ring, step):
        return index(half, step, 0) if ring == 0 else index(half, 0, step)

    def start(half, ring, q):
        for kind, step in ((0, 1), (1, -1)):
            one = copy(half, ring, kind, place(half, ring, q, 0), q == 0, peer(half, ring, step))
            one.start()
            sent.append(one)

    def relay(half, ring, q):
        for kind, step in ((0, 1), (1, -1)):
            copy(half, ring, kind, place(half, ring, q, -step), False, peer(half, ring, step)).wait_recv()
            one = copy(half, ring, kind + 2, place(half, ring, q, -step), False, peer(half, ring, step))
            one.start()
            sent.append(one)

    def finish(half, ring, q):
        for kind, step in ((2, 1), (3, -1)):
            copy(half, ring, kind, place(half, ring, q, 2), False, peer(half, ring, step)).wait_recv()

    order = ((1, 0), (2, -1), (3, 1), (4, 2))
    for half in range(2):
        start(half, 0, 0)
    for half in range(2):
        start(half, 1, 0)
    for half in range(2):
        relay(half, 0, 0)
        start(half, 2, -1)
        start(half, 3, 1)
    for half in range(2):
        relay(half, 1, 0)
    for half in range(2):
        finish(half, 0, 0)
        start(half, 4, 2)
    for ring, q in order[1:]:
        for half in range(2):
            relay(half, ring, q)
    for ring, q in order:
        for half in range(2):
            finish(half, ring, q)
    for one in sent:
        one.wait_send()


def gather_solves(own):
    depth, width = own.shape
    devices = GRID * GRID
    return pl.pallas_call(
        gather_kernel,
        out_shape=jax.ShapeDtypeStruct((devices, depth, width), own.dtype),
        in_specs=[VMEM],
        out_specs=VMEM,
        scratch_shapes=[pltpu.SemaphoreType.DMA((40,)), pltpu.SemaphoreType.DMA((40,))],
        compiler_params=pltpu.CompilerParams(
            collective_id=0, has_side_effects=True, vmem_limit_bytes=8 * MIB
        ),
        name="gather_solves",
    )(own).reshape(devices * depth, width)


def reduce_kernel(
    main_ref, extra_ref, diag_ref, both_ref, pivot_ref,
    got_main, got_extra, acc_main, acc_extra,
    main_back, main_on, extra_back, extra_on, y_slots, x_slots, stage,
    send_sem, recv_sem,
):
    chips = main_ref.shape[0]
    far = chips // 2
    scen = lax.axis_index("scen")
    me = lax.axis_index("row")
    z, core = scen // 2, scen % 2
    x, y = me // GRID, me % GRID
    partner = {"scen": z * 2 + 1 - core}
    back = {"scen": ((z + chips - 1) % chips) * 2 + core}
    on = {"scen": ((z + 1) % chips) * 2 + core}
    y_peers = [{"row": x * GRID + (y + j) % GRID} for j in range(1, GRID)]
    x_peers = [{"row": ((x + j) % GRID) * GRID + y} for j in range(1, GRID)]
    greet([partner, back, on] + y_peers + x_peers)
    sent = []
    slots = iter(range(send_sem.shape[0]))

    def copy(source, there, slot, device):
        return pltpu.make_async_remote_copy(
            src_ref=source,
            dst_ref=there,
            send_sem=send_sem.at[slot],
            recv_sem=recv_sem.at[slot],
            device_id=device,
            device_id_type=MESH,
        )

    def send(source, there, slot, device):
        one = copy(source, there, slot, device)
        one.start()
        sent.append(one)
        return one

    swap_extra = send(extra_ref.at[:, 1 - core], got_extra, next(slots), partner)
    swap_main = send(main_ref.at[:, 1 - core], got_main, next(slots), partner)

    def ring(acc, back_slots, on_slots):
        back_ids = [next(slots) for _ in range(far)]
        on_ids = [next(slots) for _ in range(far - 1)]
        back_sent, on_sent = [], []

        def step(k):
            if k <= far:
                to = (z + far + k) % chips
                if k >= 1:
                    back_sent[k - 1].wait_recv()
                    acc[to] = acc[to] + back_slots[k - 1]
                if k < far:
                    back_sent.append(send(acc.at[to], back_slots.at[k], back_ids[k], back))
            if k <= far - 1:
                to = (z + far - 1 - k) % chips
                if k >= 1:
                    on_sent[k - 1].wait_recv()
                    acc[to] = acc[to] + on_slots[k - 1]
                if k < far - 1:
                    on_sent.append(send(acc.at[to], on_slots.at[k], on_ids[k], on))

        return step

    swap_extra.wait_recv()
    acc_extra[...] = extra_ref[:, core] + got_extra[...]
    extra_step = ring(acc_extra, extra_back, extra_on)
    main_step = ring(acc_main, main_back, main_on)
    extra_step(0)
    swap_main.wait_recv()
    acc_main[...] = main_ref[:, core] + got_main[...]
    for k in range(1, far):
        extra_step(k)
    main_step(0)
    extra_step(far)
    y_sent = [
        send(acc_extra.at[z], y_slots.at[j], next(slots), device) for j, device in enumerate(y_peers)
    ]
    main_step(1)
    for one in y_sent:
        one.wait_recv()
    stage[...] = (acc_extra[z] + y_slots[0]) + (y_slots[1] + y_slots[2])
    x_sent = [
        send(stage, x_slots.at[j], next(slots), device) for j, device in enumerate(x_peers)
    ]
    main_step(2)
    for one in x_sent:
        one.wait_recv()
    pivot_ref[z, core] = (stage[...] + x_slots[0]) + (x_slots[1] + x_slots[2])

    back_ids = [next(slots) for _ in range(far)]
    on_ids = [next(slots) for _ in range(far - 1)]
    share_ids = [next(slots) for _ in range(chips)]

    def block(offset, side):
        return pivot_ref.at[(z + offset + chips) % chips, side]

    def pass_back(k, offset):
        return copy(block(offset, core), block(offset, core), back_ids[k], back)

    def pass_on(k, offset):
        return copy(block(offset, core), block(offset, core), on_ids[k], on)

    def share(offset):
        send(block(offset, core), block(offset, core), share_ids[offset + far - 1], partner)

    def launch(one):
        one.start()
        sent.append(one)

    launch(pass_back(0, 0))
    launch(pass_on(0, 0))
    share(0)
    main_step(3)
    for k in range(1, far + 1):
        pass_back(k - 1, k).wait_recv()
        if k < far:
            launch(pass_back(k, k))
        if k < far:
            pass_on(k - 1, -k).wait_recv()
            if k < far - 1:
                launch(pass_on(k, -k))
            share(-k)
        share(k)
        if k + 3 <= far:
            main_step(k + 3)
    both_ref[...] = acc_main[z] + diag_ref[...]
    for offset in range(1 - far, far + 1):
        copy(
            block(offset, 1 - core), block(offset, 1 - core), share_ids[offset + far - 1], partner
        ).wait_recv()
    for one in sent:
        one.wait_send()


def reduce_and_share(main, extra, diag):
    rows, panel = main.shape
    scens = lax.axis_size("scen")
    chips = scens // 2
    far = chips // 2
    share, pivots = rows // scens, panel // scens
    f32 = jnp.float32
    count = 2 + 3 * (2 * far - 1) + 2 * (GRID - 1) + chips
    both, pivot = pl.pallas_call(
        reduce_kernel,
        out_shape=(
            jax.ShapeDtypeStruct((share, panel), f32),
            jax.ShapeDtypeStruct((chips, 2, pivots, panel), f32),
        ),
        in_specs=[VMEM] * 3,
        out_specs=(VMEM, VMEM),
        scratch_shapes=[
            pltpu.VMEM((chips, share, panel), f32),
            pltpu.VMEM((chips, pivots, panel), f32),
            pltpu.VMEM((chips, share, panel), f32),
            pltpu.VMEM((chips, pivots, panel), f32),
            pltpu.VMEM((far, share, panel), f32),
            pltpu.VMEM((far - 1, share, panel), f32),
            pltpu.VMEM((far, pivots, panel), f32),
            pltpu.VMEM((far - 1, pivots, panel), f32),
            pltpu.VMEM((GRID - 1, pivots, panel), f32),
            pltpu.VMEM((GRID - 1, pivots, panel), f32),
            pltpu.VMEM((pivots, panel), f32),
            pltpu.SemaphoreType.DMA((count,)),
            pltpu.SemaphoreType.DMA((count,)),
        ],
        compiler_params=pltpu.CompilerParams(
            collective_id=1, has_side_effects=True, vmem_limit_bytes=16 * MIB
        ),
        name="reduce_and_share",
    )(main.reshape(chips, 2, share, panel), extra.reshape(chips, 2, pivots, panel), diag)
    return both, pivot.reshape(panel, panel)


def exact(a, b):
    return jnp.dot(a, b, precision=lax.Precision.HIGHEST, preferred_element_type=jnp.float32)


def split(a):
    high = a.astype(jnp.bfloat16)
    return high, (a - high.astype(jnp.float32)).astype(jnp.bfloat16)


def split_dot(a, b):
    def dot(p, q):
        return jnp.dot(p, q, preferred_element_type=jnp.float32)

    return dot(a[0], b[0]) + (dot(a[0], b[1]) + dot(a[1], b[0]))


def invert(pivot, approx_ref):
    size = jnp.abs(pivot)
    norm_one = jnp.max(jnp.sum(size, axis=0, keepdims=True), axis=1, keepdims=True)
    norm_inf = jnp.max(jnp.sum(size, axis=1, keepdims=True), axis=0, keepdims=True)
    approx_ref[...] = pivot.T / (norm_one * norm_inf)
    parts = split(pivot)

    def step(_, carry):
        approx = approx_ref[...]
        both = split(approx)
        left = split(split_dot(both, parts))
        approx_ref[...] = 2.0 * approx - split_dot(left, both)
        return carry

    lax.fori_loop(0, NEWTON - 1, step, 0)
    approx = approx_ref[...]
    return 2.0 * approx - exact(exact(approx, pivot), approx)


def eliminate_kernel(both_ref, pivot_ref, first_ref, second_ref, approx_ref):
    inverse_first = invert(pivot_ref[:HALF, :HALF], approx_ref)
    upper = pivot_ref[:HALF, HALF:]
    first = exact(both_ref[:, :HALF], inverse_first)
    first_ref[...] = first[:, None, :]
    lower = exact(pivot_ref[HALF:, :HALF], inverse_first)
    pivot_two = pivot_ref[HALF:, HALF:] - exact(lower, upper)
    updated = both_ref[:, HALF:] - exact(first, upper)
    second_ref[...] = exact(updated, invert(pivot_two, approx_ref))[:, None, :]


def eliminate(both, pivots):
    half = jax.ShapeDtypeStruct((both.shape[0], 1, HALF), jnp.float32)
    return pl.pallas_call(
        eliminate_kernel,
        out_shape=(half, half),
        in_specs=[VMEM, VMEM],
        out_specs=(VMEM, VMEM),
        scratch_shapes=[pltpu.VMEM((HALF, HALF), jnp.float32)],
        compiler_params=pltpu.CompilerParams(vmem_limit_bytes=16 * MIB),
        name="eliminate",
    )(both, pivots)


TILE = 256


def product_kernel(coupling_ref, solves_ref, pick_ref, diag_ref, main_ref, extra_ref, chosen_ref):
    depth, rows = coupling_ref.shape
    panel = solves_ref.shape[1]

    def dot(a, b):
        return jnp.dot(a, b, preferred_element_type=jnp.float32)

    def across(a, b):
        return lax.dot_general(a, b, (((0,), (0,)), ((), ())), preferred_element_type=jnp.float32)

    for at in range(0, depth, TILE):
        part = pl.ds(at, TILE)
        chosen_ref[part, :] = dot(coupling_ref[part, :], pick_ref[...]).astype(jnp.bfloat16)
    for at in range(0, panel, TILE):
        part = pl.ds(at, TILE)
        row = at + lax.broadcasted_iota(jnp.int32, (TILE, panel), 0)
        column = lax.broadcasted_iota(jnp.int32, (TILE, panel), 1)
        diag = jnp.where(row == column, diag_ref[part, :], jnp.float32(0.0))
        extra_ref[part, :] = across(chosen_ref[:, part], solves_ref[...]) + diag
    for at in range(0, rows, TILE):
        part = pl.ds(at, TILE)
        main_ref[part, :] = across(coupling_ref[:, part], solves_ref[...])


def products(coupling, full_solves, pick, diag):
    depth, rows = coupling.shape
    panel = full_solves.shape[1]
    return pl.pallas_call(
        product_kernel,
        out_shape=(
            jax.ShapeDtypeStruct((rows, panel), jnp.float32),
            jax.ShapeDtypeStruct((panel, panel), jnp.float32),
        ),
        in_specs=[VMEM] * 4,
        out_specs=(VMEM, VMEM),
        scratch_shapes=[pltpu.VMEM((depth, panel), jnp.bfloat16)],
        compiler_params=pltpu.CompilerParams(vmem_limit_bytes=28 * MIB),
        name="products",
    )(coupling, full_solves, pick, diag)


def shards(coupling, solves, border_diagonal, panel_rows):
    scens = lax.axis_size("scen")
    full_solves = gather_solves(solves[0])
    row_count = coupling.shape[2]
    panel = panel_rows.shape[0]
    share = row_count // scens
    first_row = lax.axis_index("row") * row_count
    base = first_row + lax.axis_index("scen") * share
    local = first_row + jnp.arange(row_count, dtype=jnp.int32)
    pick = (local[:, None] == panel_rows[None, :]).astype(jnp.bfloat16)
    glob = base + jnp.arange(share, dtype=jnp.int32)
    diag_part = jnp.where(
        glob[:, None] == panel_rows[None, :], border_diagonal[:, 0][:, None], jnp.float32(0.0)
    )
    diag_row = jnp.sum(diag_part, axis=0)[:, None]
    full_solves, diag_part, diag_row = lax.optimization_barrier((full_solves, diag_part, diag_row))
    main, extra = products(coupling[0], full_solves, pick, diag_row)
    both, pivots = reduce_and_share(main, extra, diag_part)
    return eliminate(both, pivots)


def solution(mesh):
    placed = (P("scen", None, "row"), P("scen", "row", None), P("scen", "row"), P())
    return jax.shard_map(
        shards,
        mesh=mesh,
        in_specs=placed,
        out_specs=(P("scen", "row", None), P("scen", "row", None)),
        check_vma=False,
    )
```
